32 devices in a mesh: section: 2 (over x), row: 2 (over y), col: 2 (over core), dp: 4 (over z).
Axes of the slice: x: 2, y: 2, z: 4, core: 2. Of those that a mesh axis runs over, the one named last changes fastest.
Arguments:
- hidden_in: bfloat16 [8, 256, 576], P('dp', None, ('row', 'col')), may hold values from -6 to 6
- cotangent: bfloat16 [8, 256, 576], P('dp', None, ('row', 'col')), may hold values from -6 to 6
- positions: int32 [8, 256], P('dp'), may hold values from 0 to 4861, as said below
- w_query: bfloat16 [2, 576, 2, 288], P('section', 'row', 'col'), may hold values from -16 to 16
- w_keyval: bfloat16 [2, 576, 2, 192], P('section', 'row', 'col'), may hold values from -1 to 1
- w_output: bfloat16 [2, 2, 288, 576], P('section', 'col', None, 'row'), may hold values from -1 to 1
- w_gateup: bfloat16 [2, 2, 576, 1536], P('section', None, 'row', 'col'), may hold values from -0.25 to 0.25
- w_down: bfloat16 [2, 1536, 576], P('section', 'col', 'row'), may hold values from -0.15625 to 0.15625
- norm_gains: bfloat16 [2, 2, 576], P('section', None, 'row'), may hold values from 0.5 to 1.5
Outputs:
- hidden_out: float32 [2, 8, 256, 576], P('section', 'dp', None, ('row', 'col'))
- input_grads: float32 [2, 8, 256, 576], P('section', 'dp', None, ('row', 'col'))
- d_query: float32 [2, 576, 2, 288], P('section', 'row', 'col')
- d_keyval: float32 [2, 576, 2, 192], P('section', 'row', 'col')
- d_output: float32 [2, 2, 288, 576], P('section', 'col', None, 'row')
- d_gateup: float32 [2, 2, 576, 1536], P('section', None, 'row', 'col')
- d_down: float32 [2, 1536, 576], P('section', 'col', 'row')
- d_norm_gains: float32 [2, 2, 576], P('section', None, ('row', 'col'))
The draws below stay inside these ranges and needn't reach their ends.
Inputs may be any that keep to these rules, and one draw needn't show every extreme that they name: Within each sequence the positions rise by 1 to 3 from token to token.
All inputs are finite; a program needn't handle non-finite values.
Results may differ from the reference program's by a relative error of at most 0.023.
Values may be sent and summed in bfloat16 or wider, within the bound.
A program may use at most 128 MiB of HBM per device.

```python
import math
import jax
import jax.numpy as jnp
from jax import lax

D = 576
HEADS = 9
KV_HEADS = 3
HEAD = 64
FF = 1536
SEQ = 256
LAYERS = 2
SEQS = 8
HEAD_PART = 32
N_COL = 2


def qk_pair(key):
    part_width = HEAD // N_COL
    key_kv = jax.random.fold_in(key, 101)
    key_noise = jax.random.fold_in(key, 202)
    keyval = jax.random.normal(key_kv, (LAYERS, D, N_COL, 2 * KV_HEADS * part_width), jnp.float32) * D ** (-0.5)
    noise_part = jax.random.normal(key_noise, (LAYERS, D, N_COL, HEADS, part_width), jnp.float32) * D ** (-0.5)
    query_w = noise_part
    return (query_w.reshape(LAYERS, D, N_COL, HEADS * part_width), keyval)


def draw_w_query(key, part):
    return qk_pair(key)[0].astype(jnp.bfloat16)


def draw_w_keyval(key, part):
    return qk_pair(key)[1].astype(jnp.bfloat16)


def draw_positions(key, part):
    key_off = jax.random.fold_in(key, 11)
    key_step = jax.random.fold_in(key, 22)
    offsets = jax.random.randint(key_off, (SEQS, 1), 0, 4097, dtype=jnp.int32)
    offsets = offsets.at[0, 0].set(0).at[SEQS - 1, 0].set(4096)
    steps_all = jax.random.randint(key_step, (SEQS, SEQ), 1, 4, dtype=jnp.int32)
    steps_all = steps_all.at[SEQS - 1, :].set(3)
    steps_all = steps_all.at[:, 0].set(0)
    return offsets + jnp.cumsum(steps_all, axis=1, dtype=jnp.int32)


def block_levels(key, dims, cuts, smallest, top_value):
    level = 1.0
    for position, parts in cuts:
        steps = jax.random.uniform(jax.random.fold_in(jax.random.fold_in(key, 6), position), (parts,), jnp.float32, smallest / len(cuts), top_value / len(cuts))
        level = level * jnp.repeat(jnp.exp(steps), dims[position] // parts).reshape((-1,) + (1,) * (len(dims) - 1 - position))
    return level


def noise(stream_key, shape, scale, reach, shards=(), kind=jnp.bfloat16):
    drawn = jax.random.normal(stream_key, shape, jnp.float32) * scale
    if len(shards) > 0:
        drawn = block_levels(stream_key, shape, shards, -0.22, 0.18) * drawn
    return jnp.clip(drawn, min=-reach, max=reach).astype(kind)


def setup_inputs(seed: int = 0) -> dict:
    key_list = jax.random.split(jax.random.key(seed), 10)
    hidden_in = noise(key_list[0], (SEQS, SEQ, D), 1.0, 6.0, ((0, 4), (2, 4)))
    cotangent = noise(key_list[1], (SEQS, SEQ, D), 1.0, 6.0, ((0, 4), (2, 4)))
    positions = draw_positions(jax.random.fold_in(key_list[9], 71), 0)
    w_query = draw_w_query(jax.random.fold_in(key_list[9], 71), 0)
    w_keyval = draw_w_keyval(jax.random.fold_in(key_list[9], 71), 0)
    w_output = noise(key_list[5], (LAYERS, N_COL, HEADS * HEAD_PART, D), (HEADS * HEAD // 16) ** -0.5, 1.0, ((0, 2), (1, 2), (3, 2)))
    w_gateup = noise(key_list[6], (LAYERS, 2, D, FF), D ** -0.5, 0.25, ((0, 2), (2, 2), (3, 2)))
    w_down = noise(key_list[7], (LAYERS, FF, D), FF ** -0.5, 0.15625, ((0, 2), (1, 2), (2, 2)))
    norm_gains = jnp.clip(1.0 + 0.1 * jax.random.normal(key_list[8], (LAYERS, 2, D), jnp.float32), 0.5, 1.5).astype(jnp.bfloat16)
    return dict(hidden_in=hidden_in, cotangent=cotangent, positions=positions, w_query=w_query, w_keyval=w_keyval, w_output=w_output, w_gateup=w_gateup, w_down=w_down, norm_gains=norm_gains)


EPS = 1e-05
THETA = 100000.0
MASKED = -1e+30

def rotate(values, pos_row, inverse):
    n_col_here = values.shape[1]
    half_width = values.shape[3] // 2
    freq_index = jnp.arange(n_col_here, dtype=jnp.int32)[:, None] * half_width + jnp.arange(half_width, dtype=jnp.int32)[None, :]
    freq_rates = jnp.exp(freq_index.astype(jnp.float32) * (-2.0 * math.log(THETA) / HEAD))
    angles = pos_row.astype(jnp.float32)[:, None, None] * freq_rates[None]
    cosine = jnp.cos(angles)[:, :, None, :]
    sine_part = jnp.sin(angles)[:, :, None, :]
    lower_part = values[..., :half_width]
    upper_part = values[..., half_width:]
    if inverse:
        return jnp.concatenate([lower_part * cosine + upper_part * sine_part, upper_part * cosine - lower_part * sine_part], axis=-1)
    return jnp.concatenate([lower_part * cosine - upper_part * sine_part, upper_part * cosine + lower_part * sine_part], axis=-1)

def to_heads(values):
    seqlen = values.shape[0]
    return values.transpose(0, 2, 1, 3).reshape(seqlen, values.shape[2], -1)

def lin_layout(values, n_col_here):
    seqlen = values.shape[0]
    return values.reshape(seqlen, values.shape[1], n_col_here, -1).transpose(0, 2, 1, 3)

def attention_probs(query_rot, key_rot):
    seqlen = query_rot.shape[0]
    groups = key_rot.shape[1]
    grouped = query_rot.astype(jnp.float32).reshape(seqlen, groups, HEADS // groups, -1)
    scores = jnp.einsum('qgrd,kgd->grqk', grouped, key_rot.astype(jnp.float32)) * HEAD ** (-0.5)
    token_idx = jnp.arange(seqlen)
    causal = token_idx[:, None] >= token_idx[None, :]
    scores = jnp.where(causal, scores, MASKED)
    row_top = lax.optimization_barrier(jnp.max(scores, axis=-1, keepdims=True))
    log_total = row_top + jnp.log(lax.optimization_barrier(jnp.sum(jnp.exp(scores - row_top), axis=-1, keepdims=True)))
    soft_probs = jnp.exp(scores - log_total)
    return (soft_probs, soft_probs.astype(jnp.bfloat16), grouped)

def layer_forward(hidden, pos_row, weights):
    w_q, w_kv, w_o, w_gu, w_dn, gain_pair = weights
    seqlen = hidden.shape[0]
    n_col_here = w_q.shape[1]
    head_part = w_q.shape[2] // HEADS
    gain_attn = gain_pair[0].astype(jnp.float32)
    gain_mlp = gain_pair[1].astype(jnp.float32)
    scale_attn = lax.rsqrt(lax.optimization_barrier(jnp.mean(hidden * hidden, axis=1)) + EPS)
    mixed_attn = (hidden * gain_attn).astype(jnp.bfloat16)
    query_lin = (scale_attn[:, None] * jnp.dot(mixed_attn, w_q.reshape(D, -1), preferred_element_type=jnp.float32)).reshape(seqlen, n_col_here, HEADS, head_part)
    keyval_lin = (scale_attn[:, None] * jnp.dot(mixed_attn, w_kv.reshape(D, -1), preferred_element_type=jnp.float32)).reshape(seqlen, n_col_here, 2, KV_HEADS, head_part)
    query_rot = to_heads(rotate(query_lin, pos_row, False)).astype(jnp.bfloat16)
    key_rot = to_heads(rotate(keyval_lin[:, :, 0], pos_row, False)).astype(jnp.bfloat16)
    value_rows = to_heads(keyval_lin[:, :, 1]).astype(jnp.bfloat16)
    soft_probs, probs_round, grouped = attention_probs(query_rot, key_rot)
    attended = jnp.einsum('grqk,kgd->qgrd', probs_round.astype(jnp.float32), value_rows.astype(jnp.float32)).reshape(seqlen, HEADS, -1).astype(jnp.bfloat16)
    attn_flat = lin_layout(attended, n_col_here).reshape(seqlen, -1)
    mid_resid = hidden + jnp.dot(attn_flat, w_o.reshape(-1, D), preferred_element_type=jnp.float32)
    scale_mlp = lax.rsqrt(lax.optimization_barrier(jnp.mean(mid_resid * mid_resid, axis=1)) + EPS)
    mixed_mlp = (mid_resid * gain_mlp).astype(jnp.bfloat16)
    gate_lin = scale_mlp[:, None] * jnp.dot(mixed_mlp, w_gu[0], preferred_element_type=jnp.float32)
    up_lin = scale_mlp[:, None] * jnp.dot(mixed_mlp, w_gu[1], preferred_element_type=jnp.float32)
    act_rows = (jax.nn.silu(gate_lin) * up_lin).astype(jnp.bfloat16)
    layer_out = mid_resid + jnp.dot(act_rows, w_dn, preferred_element_type=jnp.float32)
    cache = (scale_attn, mixed_attn, query_rot, key_rot, value_rows, soft_probs, probs_round, grouped, attn_flat, mid_resid, scale_mlp, mixed_mlp, gate_lin, up_lin, act_rows)
    return (layer_out, cache)

def norm_back(grad_after, resid_rows, d_mixed, gain, scale_rows):
    inner_sum = lax.optimization_barrier(jnp.sum(resid_rows * gain * d_mixed, axis=1))
    grad_new = grad_after + gain * d_mixed - resid_rows * (scale_rows * scale_rows * inner_sum / D)[:, None]
    return (grad_new, lax.optimization_barrier(jnp.sum(resid_rows * d_mixed, axis=0)))

def layer_backward(hidden, pos_row, grad_out, weights):
    w_q, w_kv, w_o, w_gu, w_dn, gain_pair = weights
    seqlen = hidden.shape[0]
    n_col_here = w_q.shape[1]
    gain_attn = gain_pair[0].astype(jnp.float32)
    gain_mlp = gain_pair[1].astype(jnp.float32)
    layer_out, cache = layer_forward(hidden, pos_row, weights)
    scale_attn, mixed_attn, query_rot, key_rot, value_rows, soft_probs, probs_round, grouped, attn_flat, mid_resid, scale_mlp, mixed_mlp, gate_lin, up_lin, act_rows = cache
    grad_round = grad_out.astype(jnp.bfloat16)
    d_down = jnp.dot(act_rows.T, grad_round, preferred_element_type=jnp.float32)
    d_act = jnp.dot(grad_round, w_dn.T, preferred_element_type=jnp.float32)
    sigmoid_gate = jax.nn.sigmoid(gate_lin)
    d_gate = d_act * up_lin * sigmoid_gate * (1.0 + gate_lin * (1.0 - sigmoid_gate))
    d_up = d_act * jax.nn.silu(gate_lin)
    d_gate_b = (scale_mlp[:, None] * d_gate).astype(jnp.bfloat16)
    d_up_b = (scale_mlp[:, None] * d_up).astype(jnp.bfloat16)
    d_gateup = jnp.stack([jnp.dot(mixed_mlp.T, d_gate_b, preferred_element_type=jnp.float32), jnp.dot(mixed_mlp.T, d_up_b, preferred_element_type=jnp.float32)])
    d_mixed_mlp = jnp.dot(d_gate_b, w_gu[0].T, preferred_element_type=jnp.float32) + jnp.dot(d_up_b, w_gu[1].T, preferred_element_type=jnp.float32)
    grad_mid, d_gain_mlp = norm_back(grad_out, mid_resid, d_mixed_mlp, gain_mlp, scale_mlp)
    mid_round = grad_mid.astype(jnp.bfloat16)
    d_output = jnp.dot(attn_flat.T, mid_round, preferred_element_type=jnp.float32).reshape(n_col_here, -1, D)
    d_attended = jnp.dot(mid_round, w_o.reshape(-1, D).T, preferred_element_type=jnp.float32).astype(jnp.bfloat16)
    d_attn_heads = to_heads(d_attended.reshape(seqlen, n_col_here, HEADS, -1))
    groups = key_rot.shape[1]
    d_grouped = d_attn_heads.astype(jnp.float32).reshape(seqlen, groups, HEADS // groups, -1)
    d_values = jnp.einsum('grqk,qgrd->kgd', probs_round.astype(jnp.float32), d_grouped)
    d_probs = jnp.einsum('qgrd,kgd->grqk', d_grouped, value_rows.astype(jnp.float32))
    d_scores = (soft_probs * (d_probs - lax.optimization_barrier(jnp.sum(soft_probs * d_probs, axis=-1, keepdims=True)))).astype(jnp.bfloat16)
    d_query = jnp.einsum('grqk,kgd->qgrd', d_scores.astype(jnp.float32), key_rot.astype(jnp.float32)).reshape(seqlen, HEADS, -1) * HEAD ** (-0.5)
    d_keys = jnp.einsum('grqk,qgrd->kgd', d_scores.astype(jnp.float32), grouped) * HEAD ** (-0.5)
    dq_lin = rotate(lin_layout(d_query, n_col_here), pos_row, True)
    dk_lin = rotate(lin_layout(d_keys, n_col_here), pos_row, True)
    dv_lin = lin_layout(d_values, n_col_here)
    d_pq = (scale_attn[:, None] * dq_lin.reshape(seqlen, -1)).astype(jnp.bfloat16)
    d_pkv = (scale_attn[:, None] * jnp.stack([dk_lin, dv_lin], axis=2).reshape(seqlen, -1)).astype(jnp.bfloat16)
    d_query_w = jnp.dot(mixed_attn.T, d_pq, preferred_element_type=jnp.float32).reshape(D, n_col_here, -1)
    d_keyval_w = jnp.dot(mixed_attn.T, d_pkv, preferred_element_type=jnp.float32).reshape(D, n_col_here, -1)
    d_mixed_attn = jnp.dot(d_pq, w_q.reshape(D, -1).T, preferred_element_type=jnp.float32) + jnp.dot(d_pkv, w_kv.reshape(D, -1).T, preferred_element_type=jnp.float32)
    grad_in, d_gain_attn = norm_back(grad_mid, hidden, d_mixed_attn, gain_attn, scale_attn)
    return (grad_in, (d_query_w, d_keyval_w, d_output, d_gateup, d_down, jnp.stack([d_gain_attn, d_gain_mlp])))

def backward_layer(inputs, pos_all, grads_out, weights):
    zero_sums = (jnp.zeros(weights[0].shape, jnp.float32), jnp.zeros(weights[1].shape, jnp.float32), jnp.zeros(weights[2].shape, jnp.float32), jnp.zeros(weights[3].shape, jnp.float32), jnp.zeros(weights[4].shape, jnp.float32), jnp.zeros(weights[5].shape, jnp.float32))

    def step_fn(totals, seq_items):
        grad_in, pieces = layer_backward(seq_items[0], seq_items[1], seq_items[2], weights)
        return (jax.tree.map(jnp.add, totals, pieces), grad_in)
    totals, grad_ins = lax.scan(step_fn, zero_sums, (inputs, pos_all, grads_out))
    return (grad_ins, totals)

def reference(hidden_in, cotangent, positions, w_query, w_keyval, w_output, w_gateup, w_down, norm_gains):
    first_w = (w_query[0], w_keyval[0], w_output[0], w_gateup[0], w_down[0], norm_gains[0])
    second_w = (w_query[1], w_keyval[1], w_output[1], w_gateup[1], w_down[1], norm_gains[1])
    start_rows = hidden_in.astype(jnp.float32)
    after_first = lax.map(lambda seq_pair: layer_forward(seq_pair[0], seq_pair[1], first_w)[0], (start_rows, positions))
    after_second = lax.map(lambda seq_pair: layer_forward(seq_pair[0], seq_pair[1], second_w)[0], (after_first, positions))
    grads_second, sums_second = backward_layer(after_first, positions, cotangent.astype(jnp.float32), second_w)
    grads_first, sums_first = backward_layer(start_rows, positions, grads_second, first_w)
    return (jnp.stack([after_first, after_second]), jnp.stack([grads_first, grads_second]), jnp.stack([sums_first[0], sums_second[0]]), jnp.stack([sums_first[1], sums_second[1]]), jnp.stack([sums_first[2], sums_second[2]]), jnp.stack([sums_first[3], sums_second[3]]), jnp.stack([sums_first[4], sums_second[4]]), jnp.stack([sums_first[5], sums_second[5]]))
```

```python
import functools
import math

import jax
import jax.numpy as jnp
from jax import lax
from jax.experimental import pallas as pl
from jax.experimental.pallas import tpu as pltpu
from jax.sharding import PartitionSpec as P

D = 576
HEADS = 9
KV_HEADS = 3
HEAD = 64
PART = 32
GROUP = HEADS // KV_HEADS
QW = HEADS * PART
KW = KV_HEADS * PART
RW = QW + KW
EPS = 1e-05
THETA = 100000.0
MASKED = -1e30
F32 = jnp.float32
BF = jnp.bfloat16


def mm(a, b, ca=1, cb=0):
    return lax.dot_general(a, b, (((ca,), (cb,)), ((), ())), preferred_element_type=F32)


def partner(x):
    width = x.shape[1]
    lane = lax.broadcasted_iota(jnp.int32, x.shape, 1)
    return jnp.where(lane % 32 < 16, pltpu.roll(x, width - 16, 1), pltpu.roll(x, 16, 1))


def inv_rms(x):
    return lax.rsqrt(jnp.mean(x * x, axis=1, keepdims=True) + EPS)


def part(x, start):
    return x[:, start : start + PART]


def pair(a, b, start):
    return jnp.concatenate([part(a, start), part(b, start)], axis=1)


def project(h, gain, cos_ref, sin_ref, wa):
    x = (h * gain).astype(BF)
    r = inv_rms(h)
    rots, vals = [], []
    for c in range(2):
        lin = r * mm(x, wa[c][...])
        qk = lin[:, :RW]
        rots.append((qk * cos_ref[c] + partner(qk) * sin_ref[c]).astype(BF))
        vals.append(lin[:, RW:].astype(BF))
    return x, r, rots, vals


def group_probs(g, rots, vals):
    k = pair(rots[0], rots[1], QW + g * PART)
    v = pair(vals[0], vals[1], g * PART)
    q = jnp.concatenate(
        [pair(rots[0], rots[1], (g * GROUP + i) * PART) for i in range(GROUP)], axis=0
    )
    s = mm(q, k, 1, 1) * HEAD ** (-0.5)
    tokens = k.shape[0]
    row = lax.broadcasted_iota(jnp.int32, s.shape, 0) % tokens
    col = lax.broadcasted_iota(jnp.int32, s.shape, 1)
    s = jnp.where(row >= col, s, MASKED)
    e = jnp.exp(s - jnp.max(s, axis=1, keepdims=True))
    p = e / jnp.sum(e, axis=1, keepdims=True)
    return q, k, v, p


def attn_fwd_kernel(h_ref, gain_ref, cos_ref, sin_ref, wa0, wa1, wo0, wo1, mid_ref):
    h = h_ref[...]
    tokens = h.shape[0]
    _, _, rots, vals = project(h, gain_ref[0:1, :], cos_ref, sin_ref, (wa0, wa1))
    heads = []
    for g in range(KV_HEADS):
        _, _, v, p = group_probs(g, rots, vals)
        o = mm(p.astype(BF), v).astype(BF)
        heads += [o[i * tokens : (i + 1) * tokens] for i in range(GROUP)]
    a0 = jnp.concatenate([o[:, :PART] for o in heads], axis=1)
    a1 = jnp.concatenate([o[:, PART:] for o in heads], axis=1)
    mid_ref[...] = h + mm(a0, wo0[...]) + mm(a1, wo1[...])


def mlp_fwd_kernel(mid_ref, gain_ref, wg0, wg1, wd0, wd1, out_ref, outb_ref):
    mid = mid_ref[...]
    x = (mid * gain_ref[1:2, :]).astype(BF)
    r = inv_rms(mid)
    total = mid
    for wg, wd in ((wg0, wd0), (wg1, wd1)):
        gate = r * mm(x, wg[0])
        up = r * mm(x, wg[1])
        act = (gate * jax.nn.sigmoid(gate) * up).astype(BF)
        total = total + mm(act, wd[...])
    out_ref[...] = total
    outb_ref[...] = total.astype(BF)


def mlp_bwd_kernel(
    mid_ref, g_ref, gain_ref, wg0, wg1, wd0, wd1, gmid_ref, *save_refs
):
    mid = mid_ref[...]
    gout = g_ref[...].astype(F32)
    gb = gout.astype(BF)
    gain = gain_ref[1:2, :]
    x = (mid * gain).astype(BF)
    r = inv_rms(mid)
    dx = None
    for c, (wg, wd) in enumerate(((wg0, wd0), (wg1, wd1))):
        gate = r * mm(x, wg[0])
        up = r * mm(x, wg[1])
        dact = mm(gb, wd[...], 1, 1)
        s = jax.nn.sigmoid(gate)
        silu = gate * s
        dgate = (r * (dact * up * s * (1.0 + gate * (1.0 - s)))).astype(BF)
        dup = (r * (dact * silu)).astype(BF)
        term = mm(dgate, wg[0], 1, 1) + mm(dup, wg[1], 1, 1)
        dx = term if dx is None else dx + term
        if save_refs and c == 0:
            x_ref, gb_ref, act_ref, dpm_ref, _ = save_refs
            x_ref[...] = x
            gb_ref[...] = gb
            act_ref[...] = (silu * up).astype(BF)
            dpm_ref[0] = dgate
            dpm_ref[1] = dup
    inner = jnp.sum(mid * gain * dx, axis=1, keepdims=True)
    gmid_ref[...] = gout + gain * dx - mid * (r * r * inner / D)
    if save_refs:
        save_refs[4][...] = jnp.sum(mid * dx, axis=0, keepdims=True)


def attn_bwd_kernel(
    h_ref, gmid_ref, gain_ref, cos_ref, sin_ref, wa0, wa1, wo0, wo1, gin_ref, ginb_ref, *save_refs
):
    h = h_ref[...]
    gmid = gmid_ref[...]
    gain = gain_ref[0:1, :]
    tokens = h.shape[0]
    x, r, rots, vals = project(h, gain, cos_ref, sin_ref, (wa0, wa1))
    mb = gmid.astype(BF)
    dv0 = mm(mb, wo0[...], 1, 1).astype(BF)
    dv1 = mm(mb, wo1[...], 1, 1).astype(BF)
    attn0, dq, dk, dv = [], [], [], []
    for g in range(KV_HEADS):
        q, k, v, p = group_probs(g, rots, vals)
        pb = p.astype(BF)
        do = jnp.concatenate(
            [pair(dv0, dv1, (g * GROUP + i) * PART) for i in range(GROUP)], axis=0
        )
        if save_refs:
            o = mm(pb, v).astype(BF)
            attn0 += [o[i * tokens : (i + 1) * tokens, :PART] for i in range(GROUP)]
        dv.append(mm(pb, do, 0, 0))
        dp = mm(do, v, 1, 1)
        ds = (p * (dp - jnp.sum(p * dp, axis=1, keepdims=True))).astype(BF)
        dqg = mm(ds, k) * HEAD ** (-0.5)
        dq += [dqg[i * tokens : (i + 1) * tokens] for i in range(GROUP)]
        dk.append(mm(ds, q, 0, 0) * HEAD ** (-0.5))
    dx = None
    for c, wa in enumerate((wa0, wa1)):
        piece = [y[:, c * PART : (c + 1) * PART] for y in dq + dk]
        dqk = jnp.concatenate(piece, axis=1)
        dqk = dqk * cos_ref[c] - partner(dqk) * sin_ref[c]
        dvc = jnp.concatenate([y[:, c * PART : (c + 1) * PART] for y in dv], axis=1)
        dpa = (r * jnp.concatenate([dqk, dvc], axis=1)).astype(BF)
        term = mm(dpa, wa[...], 1, 1)
        dx = term if dx is None else dx + term
        if save_refs and c == 0:
            save_refs[3][...] = dpa
    inner = jnp.sum(h * gain * dx, axis=1, keepdims=True)
    gin = gmid + gain * dx - h * (r * r * inner / D)
    gin_ref[...] = gin
    ginb_ref[...] = gin.astype(BF)
    if save_refs:
        save_refs[0][...] = x
        save_refs[1][...] = mb
        save_refs[2][...] = jnp.concatenate(attn0, axis=1)
        save_refs[4][...] = jnp.sum(h * dx, axis=0, keepdims=True)


def mlp_dw_kernel(x_ref, gb_ref, act_ref, dpm_ref, dg_mine, dg_other, dd_mine, dd_other):
    half = dg_mine.shape[1]
    dd = mm(act_ref[...], gb_ref[...], 0, 0).astype(BF)
    dd_mine[...] = dd[:, :half]
    dd_other[...] = dd[:, half:]
    for i in range(2):
        dg = mm(x_ref[...], dpm_ref[i], 0, 0).astype(BF)
        dg_mine[i] = dg[:half]
        dg_other[i] = dg[half:]


def attn_dw_kernel(x_ref, mb_ref, at_ref, dpa_ref, da_mine, da_other, do_mine, do_other):
    half = da_mine.shape[0]
    do = mm(at_ref[...], mb_ref[...], 0, 0).astype(BF)
    do_mine[...] = do[:, :half]
    do_other[...] = do[:, half:]
    da = mm(x_ref[...], dpa_ref[...], 0, 0).astype(BF)
    da_mine[...] = da[:half]
    da_other[...] = da[half:]


def call(kernel, outs, flops, *args):
    nbytes = sum(a.size * a.dtype.itemsize for a in args)
    return pl.pallas_call(
        kernel,
        out_shape=[jax.ShapeDtypeStruct(s, d) for s, d in outs],
        in_specs=[pl.BlockSpec(memory_space=pltpu.VMEM)] * len(args),
        out_specs=[pl.BlockSpec(memory_space=pltpu.VMEM)] * len(outs),
        compiler_params=pltpu.CompilerParams(vmem_limit_bytes=60 << 20),
        cost_estimate=pl.CostEstimate(
            flops=int(flops), bytes_accessed=nbytes, transcendentals=0
        ),
    )(*args)


def swap(x, axis):
    count = lax.axis_size(axis)
    return lax.ppermute(x, axis, [(i, count - 1 - i) for i in range(count)])


def per_device(
    hidden_in, cotangent, positions, w_query, w_keyval, w_output, w_gateup, w_down, norm_gains
):
    seqs, tokens, quarter = hidden_in.shape
    ff = w_down.shape[1]
    half = w_query.shape[1]
    assert lax.axis_size("row") == 2 and lax.axis_size("col") == 2 and seqs == 2
    section = lax.axis_index("section")
    row = lax.axis_index("row")
    col = lax.axis_index("col")
    first_col = col == 0

    both = jnp.concatenate([hidden_in, cotangent], axis=1)
    own = lax.dynamic_index_in_dim(both, row, 0, keepdims=False)
    away = lax.dynamic_index_in_dim(both, 1 - row, 0, keepdims=False)
    across = jnp.concatenate([own, swap(away, "row")], axis=0)
    beside = swap(across, "col")
    low = jnp.where(first_col, across, beside)
    high = jnp.where(first_col, beside, across)
    n2 = 2 * tokens
    full = jnp.concatenate([low[:n2], high[:n2], low[n2:], high[n2:]], axis=1)
    h0 = full[:tokens].astype(F32)
    cot = full[tokens:]

    w_attn = jnp.concatenate([w_query[0, :, 0, :], w_keyval[0, :, 0, :]], axis=1)
    gains = jnp.concatenate([norm_gains[0], swap(norm_gains[0], "row")], axis=1).astype(F32)
    wa0 = jnp.concatenate([w_attn, swap(w_attn, "row")], axis=0)
    wa1 = swap(wa0, "col")
    wo0 = jnp.concatenate([w_output[0, 0], swap(w_output[0, 0], "row")], axis=1)
    wo1 = swap(wo0, "col")
    wg0 = jnp.concatenate([w_gateup[0], swap(w_gateup[0], "row")], axis=1)
    wg1 = swap(wg0, "col")
    wd0 = jnp.concatenate([w_down[0], swap(w_down[0], "row")], axis=1)
    wd1 = swap(wd0, "col")

    pos = lax.dynamic_index_in_dim(positions, row, 0, keepdims=False).astype(F32)
    lane = jnp.arange(PART, dtype=jnp.int32)
    cols = jnp.stack([col, 1 - col]).astype(jnp.int32)
    freq_index = (cols[:, None] * (PART // 2) + lane[None, :] % (PART // 2)).astype(F32)
    rates = jnp.exp(freq_index * (-2.0 * math.log(THETA) / HEAD))
    angles = pos[None, :, None] * rates[:, None, :]
    sign = jnp.where(lane < PART // 2, -1.0, 1.0).astype(F32)
    cos = jnp.tile(jnp.cos(angles), (1, 1, RW // PART))
    sin = jnp.tile(jnp.sin(angles) * sign, (1, 1, RW // PART))

    wa, wm = (wa0, wa1, wo0, wo1), (wg0, wg1, wd0, wd1)
    tok = (tokens, D)
    flops_a = 2 * tokens * D * (RW + KW) * 2 + 2 * tokens * D * D + 4 * tokens * tokens * D
    flops_m = 2 * tokens * D * 3 * 2 * ff

    def forward(h):
        (mid,) = call(attn_fwd_kernel, [(tok, F32)], flops_a, h, gains, cos, sin, *wa)
        out, outb = call(mlp_fwd_kernel, [(tok, F32), (tok, BF)], flops_m, mid, gains, *wm)
        return mid, out, outb

    def step(x, by):
        return lax.ppermute(x, "section", [(0, 1)] if by > 0 else [(1, 0)])

    _, _, sent = forward(h0)
    h = jnp.where(section == 0, h0, step(sent, 1).astype(F32))
    mid, out, _ = forward(h)

    gmid, = call(
        mlp_bwd_kernel, [(tok, F32)], 2.7 * flops_m, mid, cot, gains, *wm
    )
    _, ginb = call(
        attn_bwd_kernel, [(tok, F32), (tok, BF)], 3 * flops_a, h, gmid, gains, cos, sin, *wa
    )
    g = jnp.where(section == 1, cot, step(ginb, -1))
    gmid, xm, gb, act, dpm, dgain_m = call(
        mlp_bwd_kernel,
        [
            (tok, F32),
            (tok, BF),
            (tok, BF),
            ((tokens, ff), BF),
            ((2, tokens, ff), BF),
            ((1, D), F32),
        ],
        2.7 * flops_m,
        mid,
        g,
        gains,
        *wm,
    )
    dg_mine, dg_other, dd_mine, dd_other = call(
        mlp_dw_kernel,
        [((2, half, ff), BF)] * 2 + [((ff, half), BF)] * 2,
        flops_m // 2,
        xm,
        gb,
        act,
        dpm,
    )
    gin, _, xa, mb, at0, dpa, dgain_a = call(
        attn_bwd_kernel,
        [
            (tok, F32),
            (tok, BF),
            (tok, BF),
            (tok, BF),
            ((tokens, QW), BF),
            ((tokens, RW + KW), BF),
            ((1, D), F32),
        ],
        3 * flops_a,
        h,
        gmid,
        gains,
        cos,
        sin,
        *wa,
    )
    da_mine, da_other, do_mine, do_other = call(
        attn_dw_kernel,
        [((half, RW + KW), BF)] * 2 + [((QW, half), BF)] * 2,
        flops_a // 2,
        xa,
        mb,
        at0,
        dpa,
    )

    def joined(mine, other):
        return (mine.astype(F32) + swap(other, "row").astype(F32)).astype(BF)

    dd, dg = lax.psum((joined(dd_mine, dd_other), joined(dg_mine, dg_other)), "dp")
    dgain = jnp.concatenate([dgain_a, dgain_m], axis=0)
    dgain = dgain[:, :half] + swap(dgain[:, half:], "row")
    dgain = jnp.where(first_col, dgain[:, :quarter], dgain[:, quarter:])
    da, do, dn = lax.psum((joined(da_mine, da_other), joined(do_mine, do_other), dgain), "dp")

    def home(x):
        mine = jnp.where(first_col, x[:, :quarter], x[:, quarter:half])
        other = jnp.where(first_col, x[:, half : half + quarter], x[:, half + quarter :])
        got = swap(other, "row")
        return jnp.where(row == 0, jnp.stack([mine, got]), jnp.stack([got, mine]))[None]

    return (
        home(out),
        home(gin),
        da[:, :QW].astype(F32).reshape(1, half, 1, QW),
        da[:, QW:].astype(F32).reshape(1, half, 1, 2 * KW),
        do.astype(F32)[None, None],
        dg.astype(F32)[None],
        dd.astype(F32)[None],
        dn[None],
    )


def solution(mesh):
    return jax.shard_map(
        per_device,
        mesh=mesh,
        in_specs=(
            P("dp", None, ("row", "col")),
            P("dp", None, ("row", "col")),
            P("dp", None),
            P("section", "row", "col", None),
            P("section", "row", "col", None),
            P("section", "col", None, "row"),
            P("section", None, "row", "col"),
            P("section", "col", "row"),
            P("section", None, "row"),
        ),
        out_specs=(
            P("section", "dp", None, ("row", "col")),
            P("section", "dp", None, ("row", "col")),
            P("section", "row", "col", None),
            P("section", "row", "col", None),
            P("section", "col", None, "row"),
            P("section", None, "row", "col"),
            P("section", "col", "row"),
            P("section", None, ("row", "col")),
        ),
        check_vma=False,
    )
```

```python
import functools
import math

import jax
import jax.numpy as jnp
from jax import lax
from jax.experimental import pallas as pl
from jax.experimental.pallas import tpu as pltpu
from jax.sharding import PartitionSpec as P

D = 576
HEADS = 9
KV_HEADS = 3
HEAD = 64
PART = 32
GROUP = HEADS // KV_HEADS
QW = HEADS * PART
KW = KV_HEADS * PART
RW = QW + KW
EPS = 1e-05
THETA = 100000.0
MASKED = -1e30
F32 = jnp.float32
BF = jnp.bfloat16


def mm(a, b, ca=1, cb=0):
    return lax.dot_general(a, b, (((ca,), (cb,)), ((), ())), preferred_element_type=F32)


def partner(x):
    width = x.shape[1]
    lane = lax.broadcasted_iota(jnp.int32, x.shape, 1)
    return jnp.where(lane % 32 < 16, pltpu.roll(x, width - 16, 1), pltpu.roll(x, 16, 1))


def inv_rms(x):
    return lax.rsqrt(jnp.mean(x * x, axis=1, keepdims=True) + EPS)


def part(x, start):
    return x[:, start : start + PART]


def pair(a, b, start):
    return jnp.concatenate([part(a, start), part(b, start)], axis=1)


def project(h, gain, cos_ref, sin_ref, wa):
    x = (h * gain).astype(BF)
    r = inv_rms(h)
    rots, vals = [], []
    for c in range(2):
        lin = r * mm(x, wa[c][...])
        qk = lin[:, :RW]
        rots.append((qk * cos_ref[c] + partner(qk) * sin_ref[c]).astype(BF))
        vals.append(lin[:, RW:].astype(BF))
    return x, r, rots, vals


def group_probs(g, rots, vals):
    k = pair(rots[0], rots[1], QW + g * PART)
    v = pair(vals[0], vals[1], g * PART)
    q = jnp.concatenate(
        [pair(rots[0], rots[1], (g * GROUP + i) * PART) for i in range(GROUP)], axis=0
    )
    s = mm(q, k, 1, 1) * HEAD ** (-0.5)
    tokens = k.shape[0]
    row = lax.broadcasted_iota(jnp.int32, s.shape, 0) % tokens
    col = lax.broadcasted_iota(jnp.int32, s.shape, 1)
    s = jnp.where(row >= col, s, MASKED)
    e = jnp.exp(s - jnp.max(s, axis=1, keepdims=True))
    p = e / jnp.sum(e, axis=1, keepdims=True)
    return q, k, v, p


def attn_fwd_kernel(h_ref, gain_ref, cos_ref, sin_ref, wa0, wa1, wo0, wo1, mid_ref):
    h = h_ref[...]
    tokens = h.shape[0]
    _, _, rots, vals = project(h, gain_ref[0:1, :], cos_ref, sin_ref, (wa0, wa1))
    heads = []
    for g in range(KV_HEADS):
        _, _, v, p = group_probs(g, rots, vals)
        o = mm(p.astype(BF), v).astype(BF)
        heads += [o[i * tokens : (i + 1) * tokens] for i in range(GROUP)]
    a0 = jnp.concatenate([o[:, :PART] for o in heads], axis=1)
    a1 = jnp.concatenate([o[:, PART:] for o in heads], axis=1)
    mid_ref[...] = h + mm(a0, wo0[...]) + mm(a1, wo1[...])


def mlp_fwd_kernel(mid_ref, gain_ref, wg0, wg1, wd0, wd1, out_ref, outb_ref):
    mid = mid_ref[...]
    x = (mid * gain_ref[1:2, :]).astype(BF)
    r = inv_rms(mid)
    total = mid
    for wg, wd in ((wg0, wd0), (wg1, wd1)):
        gate = r * mm(x, wg[0])
        up = r * mm(x, wg[1])
        act = (gate * jax.nn.sigmoid(gate) * up).astype(BF)
        total = total + mm(act, wd[...], 1, 1)
    out_ref[...] = total
    outb_ref[...] = total.astype(BF)


def mlp_bwd_kernel(
    mid_ref, g_ref, gain_ref, wg0, wg1, wd0, wd1, gmid_ref, *save_refs
):
    mid = mid_ref[...]
    gout = g_ref[...].astype(F32)
    gb = gout.astype(BF)
    gain = gain_ref[1:2, :]
    x = (mid * gain).astype(BF)
    r = inv_rms(mid)
    dx = None
    for c, (wg, wd) in enumerate(((wg0, wd0), (wg1, wd1))):
        gate = r * mm(x, wg[0])
        up = r * mm(x, wg[1])
        dact = mm(gb, wd[...])
        s = jax.nn.sigmoid(gate)
        silu = gate * s
        dgate = (r * (dact * up * s * (1.0 + gate * (1.0 - s)))).astype(BF)
        dup = (r * (dact * silu)).astype(BF)
        term = mm(dgate, wg[0], 1, 1) + mm(dup, wg[1], 1, 1)
        dx = term if dx is None else dx + term
        if save_refs and c == 0:
            x_ref, gb_ref, act_ref, dpm_ref, _ = save_refs
            x_ref[...] = x
            gb_ref[...] = gb
            act_ref[...] = (silu * up).astype(BF)
            dpm_ref[0] = dgate
            dpm_ref[1] = dup
    inner = jnp.sum(mid * gain * dx, axis=1, keepdims=True)
    gmid_ref[...] = gout + gain * dx - mid * (r * r * inner / D)
    if save_refs:
        save_refs[4][...] = jnp.sum(mid * dx, axis=0, keepdims=True)


def attn_bwd_kernel(
    h_ref, gmid_ref, gain_ref, cos_ref, sin_ref, wa0, wa1, wo0, wo1, gin_ref, ginb_ref, *save_refs
):
    h = h_ref[...]
    gmid = gmid_ref[...]
    gain = gain_ref[0:1, :]
    tokens = h.shape[0]
    x, r, rots, vals = project(h, gain, cos_ref, sin_ref, (wa0, wa1))
    mb = gmid.astype(BF)
    dv0 = mm(mb, wo0[...], 1, 1).astype(BF)
    dv1 = mm(mb, wo1[...], 1, 1).astype(BF)
    attn0, dq, dk, dv = [], [], [], []
    for g in range(KV_HEADS):
        q, k, v, p = group_probs(g, rots, vals)
        pb = p.astype(BF)
        do = jnp.concatenate(
            [pair(dv0, dv1, (g * GROUP + i) * PART) for i in range(GROUP)], axis=0
        )
        if save_refs:
            o = mm(pb, v).astype(BF)
            attn0 += [o[i * tokens : (i + 1) * tokens, :PART] for i in range(GROUP)]
        dv.append(mm(pb, do, 0, 0))
        dp = mm(do, v, 1, 1)
        ds = (p * (dp - jnp.sum(p * dp, axis=1, keepdims=True))).astype(BF)
        dqg = mm(ds, k) * HEAD ** (-0.5)
        dq += [dqg[i * tokens : (i + 1) * tokens] for i in range(GROUP)]
        dk.append(mm(ds, q, 0, 0) * HEAD ** (-0.5))
    dx = None
    for c, wa in enumerate((wa0, wa1)):
        piece = [y[:, c * PART : (c + 1) * PART] for y in dq + dk]
        dqk = jnp.concatenate(piece, axis=1)
        dqk = dqk * cos_ref[c] - partner(dqk) * sin_ref[c]
        dvc = jnp.concatenate([y[:, c * PART : (c + 1) * PART] for y in dv], axis=1)
        dpa = (r * jnp.concatenate([dqk, dvc], axis=1)).astype(BF)
        term = mm(dpa, wa[...], 1, 1)
        dx = term if dx is None else dx + term
        if save_refs and c == 0:
            save_refs[3][...] = dpa
    inner = jnp.sum(h * gain * dx, axis=1, keepdims=True)
    gin = gmid + gain * dx - h * (r * r * inner / D)
    gin_ref[...] = gin
    ginb_ref[...] = gin.astype(BF)
    if save_refs:
        save_refs[0][...] = x
        save_refs[1][...] = mb
        save_refs[2][...] = jnp.concatenate(attn0, axis=1)
        save_refs[4][...] = jnp.sum(h * dx, axis=0, keepdims=True)


def mlp_dw_kernel(x_ref, gb_ref, act_ref, dpm_ref, dg_mine, dg_other, dd_mine, dd_other):
    half = dg_mine.shape[1]
    dd = mm(gb_ref[...], act_ref[...], 0, 0).astype(BF)
    dd_mine[...] = dd[:half]
    dd_other[...] = dd[half:]
    for i in range(2):
        dg = mm(x_ref[...], dpm_ref[i], 0, 0).astype(BF)
        dg_mine[i] = dg[:half]
        dg_other[i] = dg[half:]


def attn_dw_kernel(x_ref, mb_ref, at_ref, dpa_ref, da_mine, da_other, do_mine, do_other):
    half = da_mine.shape[0]
    do = mm(at_ref[...], mb_ref[...], 0, 0).astype(BF)
    do_mine[...] = do[:, :half]
    do_other[...] = do[:, half:]
    da = mm(x_ref[...], dpa_ref[...], 0, 0).astype(BF)
    da_mine[...] = da[:half]
    da_other[...] = da[half:]


def call(kernel, outs, flops, *args):
    nbytes = sum(a.size * a.dtype.itemsize for a in args)
    return pl.pallas_call(
        kernel,
        out_shape=[jax.ShapeDtypeStruct(s, d) for s, d in outs],
        in_specs=[pl.BlockSpec(memory_space=pltpu.VMEM)] * len(args),
        out_specs=[pl.BlockSpec(memory_space=pltpu.VMEM)] * len(outs),
        compiler_params=pltpu.CompilerParams(vmem_limit_bytes=60 << 20),
        cost_estimate=pl.CostEstimate(
            flops=int(flops), bytes_accessed=nbytes, transcendentals=0
        ),
    )(*args)


def swap(x, axis):
    count = lax.axis_size(axis)
    return lax.ppermute(x, axis, [(i, count - 1 - i) for i in range(count)])


def per_device(
    hidden_in, cotangent, positions, w_query, w_keyval, w_output, w_gateup, w_down, norm_gains
):
    seqs, tokens, quarter = hidden_in.shape
    ff = w_down.shape[1]
    half = w_query.shape[1]
    assert lax.axis_size("row") == 2 and lax.axis_size("col") == 2 and seqs == 2
    section = lax.axis_index("section")
    row = lax.axis_index("row")
    col = lax.axis_index("col")
    first_col = col == 0

    both = jnp.concatenate([hidden_in, cotangent], axis=1)
    w_attn = jnp.concatenate([w_query[0, :, 0, :], w_keyval[0, :, 0, :]], axis=1)
    own = lax.dynamic_index_in_dim(both, row, 0, keepdims=False)
    away = lax.dynamic_index_in_dim(both, 1 - row, 0, keepdims=False)
    wa_got = swap(w_attn, "row")
    w_out = w_output[0, 0]
    wo_got = swap(w_out, "row")
    away = swap(away, "row")
    w_mlp, w_back, away, wa_got = lax.optimization_barrier(
        (w_gateup[0], w_down[0].T, away, wa_got)
    )
    wg_got = swap(w_mlp, "row")
    wd_got = swap(w_back, "row")
    across = jnp.concatenate([own, away], axis=0)
    beside = swap(across, "col")
    low = jnp.where(first_col, across, beside)
    high = jnp.where(first_col, beside, across)
    n2 = 2 * tokens
    full = jnp.concatenate([low[:n2], high[:n2], low[n2:], high[n2:]], axis=1)
    h0 = full[:tokens].astype(F32)
    cot = full[tokens:]

    gains = jnp.concatenate([norm_gains[0], swap(norm_gains[0], "row")], axis=1).astype(F32)
    wa0 = jnp.concatenate([w_attn, wa_got], axis=0)
    wa1 = swap(wa0, "col")
    wo0 = jnp.concatenate([w_out, wo_got], axis=1)
    wo1 = swap(wo0, "col")

    pos = lax.dynamic_index_in_dim(positions, row, 0, keepdims=False).astype(F32)
    lane = jnp.arange(PART, dtype=jnp.int32)
    cols = jnp.stack([col, 1 - col]).astype(jnp.int32)
    freq_index = (cols[:, None] * (PART // 2) + lane[None, :] % (PART // 2)).astype(F32)
    rates = jnp.exp(freq_index * (-2.0 * math.log(THETA) / HEAD))
    angles = pos[None, :, None] * rates[:, None, :]
    sign = jnp.where(lane < PART // 2, -1.0, 1.0).astype(F32)
    cos = jnp.tile(jnp.cos(angles), (1, 1, RW // PART))
    sin = jnp.tile(jnp.sin(angles) * sign, (1, 1, RW // PART))

    wa = (wa0, wa1, wo0, wo1)
    tok = (tokens, D)
    flops_a = 2 * tokens * D * (RW + KW) * 2 + 2 * tokens * D * D + 4 * tokens * tokens * D
    flops_m = 2 * tokens * D * 3 * 2 * ff

    def attn_forward(h):
        return call(attn_fwd_kernel, [(tok, F32)], flops_a, h, gains, cos, sin, *wa)[0]

    mid = attn_forward(h0)
    mid, wg_got, wd_got = lax.optimization_barrier((mid, wg_got, wd_got))
    wg0 = jnp.concatenate([w_mlp, wg_got], axis=1)
    wg1 = swap(wg0, "col")
    wd0 = jnp.concatenate([w_back, wd_got], axis=0)
    wd1 = swap(wd0, "col")
    wm = (wg0, wg1, wd0, wd1)

    def mlp_forward(mid):
        return call(mlp_fwd_kernel, [(tok, F32), (tok, BF)], flops_m, mid, gains, *wm)

    def step(x, by):
        return lax.ppermute(x, "section", [(0, 1)] if by > 0 else [(1, 0)])

    _, sent = mlp_forward(mid)
    h = jnp.where(section == 0, h0, step(sent, 1).astype(F32))
    mid = attn_forward(h)
    out, _ = mlp_forward(mid)

    gmid, = call(
        mlp_bwd_kernel, [(tok, F32)], 2.7 * flops_m, mid, cot, gains, *wm
    )
    _, ginb = call(
        attn_bwd_kernel, [(tok, F32), (tok, BF)], 3 * flops_a, h, gmid, gains, cos, sin, *wa
    )
    came, out = lax.optimization_barrier((step(ginb, -1), out))
    g = jnp.where(section == 1, cot, came)
    gmid, xm, gb, act, dpm, dgain_m = call(
        mlp_bwd_kernel,
        [
            (tok, F32),
            (tok, BF),
            (tok, BF),
            ((tokens, ff), BF),
            ((2, tokens, ff), BF),
            ((1, D), F32),
        ],
        2.7 * flops_m,
        mid,
        g,
        gains,
        *wm,
    )
    dg_mine, dg_other, dd_mine, dd_other = call(
        mlp_dw_kernel,
        [((2, half, ff), BF)] * 2 + [((half, ff), BF)] * 2,
        flops_m // 2,
        xm,
        gb,
        act,
        dpm,
    )
    dg_got, dd_got = swap(dg_other, "row"), swap(dd_other, "row")
    gmid, dg_other, dd_other = lax.optimization_barrier((gmid, dg_other, dd_other))
    gin, _, xa, mb, at0, dpa, dgain_a = call(
        attn_bwd_kernel,
        [
            (tok, F32),
            (tok, BF),
            (tok, BF),
            (tok, BF),
            ((tokens, QW), BF),
            ((tokens, RW + KW), BF),
            ((1, D), F32),
        ],
        3 * flops_a,
        h,
        gmid,
        gains,
        cos,
        sin,
        *wa,
    )
    da_mine, da_other, do_mine, do_other = call(
        attn_dw_kernel,
        [((half, RW + KW), BF)] * 2 + [((QW, half), BF)] * 2,
        flops_a // 2,
        xa,
        mb,
        at0,
        dpa,
    )

    def joined(mine, got):
        return (mine.astype(F32) + got.astype(F32)).astype(BF)

    da_got, do_got = swap(da_other, "row"), swap(do_other, "row")
    dgain = jnp.concatenate([dgain_a, dgain_m], axis=0)
    dgain = dgain[:, :half] + swap(dgain[:, half:], "row")
    dgain = jnp.where(first_col, dgain[:, :quarter], dgain[:, quarter:]).astype(BF)
    dd, dg = lax.psum((joined(dd_mine, dd_got), joined(dg_mine, dg_got)), "dp")
    rest = jnp.concatenate([joined(do_mine, do_got), dgain.reshape(1, half)], axis=0)
    late = (joined(da_mine, da_got), rest)
    late, dd, dg = lax.optimization_barrier((late, dd, dg))
    da, rest = lax.psum(late, "dp")
    do, dn = rest[:QW], rest[QW:].reshape(2, quarter)

    def home(x):
        mine = jnp.where(first_col, x[:, :quarter], x[:, quarter:half])
        other = jnp.where(first_col, x[:, half : half + quarter], x[:, half + quarter :])
        got = swap(other.astype(BF), "row").astype(F32)
        return jnp.where(row == 0, jnp.stack([mine, got]), jnp.stack([got, mine]))[None]

    return (
        home(out),
        home(gin),
        da[:, :QW].astype(F32).reshape(1, half, 1, QW),
        da[:, QW:].astype(F32).reshape(1, half, 1, 2 * KW),
        do.astype(F32)[None, None],
        dg.astype(F32)[None],
        dd.astype(F32).T[None],
        dn.astype(F32)[None],
    )


def solution(mesh):
    return jax.shard_map(
        per_device,
        mesh=mesh,
        in_specs=(
            P("dp", None, ("row", "col")),
            P("dp", None, ("row", "col")),
            P("dp", None),
            P("section", "row", "col", None),
            P("section", "row", "col", None),
            P("section", "col", None, "row"),
            P("section", None, "row", "col"),
            P("section", "col", "row"),
            P("section", None, "row"),
        ),
        out_specs=(
            P("section", "dp", None, ("row", "col")),
            P("section", "dp", None, ("row", "col")),
            P("section", "row", "col", None),
            P("section", "row", "col", None),
            P("section", "col", None, "row"),
            P("section", None, "row", "col"),
            P("section", "col", "row"),
            P("section", None, ("row", "col")),
        ),
        check_vma=False,
    )
```

```python
import functools
import math

import jax
import jax.numpy as jnp
from jax import lax
from jax.experimental import pallas as pl
from jax.experimental.pallas import tpu as pltpu
from jax.sharding import PartitionSpec as P

D = 576
HEADS = 9
KV_HEADS = 3
HEAD = 64
PART = 32
GROUP = HEADS // KV_HEADS
QW = HEADS * PART
KW = KV_HEADS * PART
RW = QW + KW
EPS = 1e-05
THETA = 100000.0
MASKED = -1e30
F32 = jnp.float32
BF = jnp.bfloat16


def mm(a, b, ca=1, cb=0):
    return lax.dot_general(a, b, (((ca,), (cb,)), ((), ())), preferred_element_type=F32)


def partner(x):
    width = x.shape[1]
    lane = lax.broadcasted_iota(jnp.int32, x.shape, 1)
    return jnp.where(lane % 32 < 16, pltpu.roll(x, width - 16, 1), pltpu.roll(x, 16, 1))


def inv_rms(x):
    return lax.rsqrt(jnp.mean(x * x, axis=1, keepdims=True) + EPS)


def part(x, start):
    return x[:, start : start + PART]


def pair(a, b, start):
    return jnp.concatenate([part(a, start), part(b, start)], axis=1)


def project(h, gain, cos_ref, sin_ref, wa):
    x = (h * gain).astype(BF)
    r = inv_rms(h)
    rots, vals = [], []
    for c in range(2):
        lin = r * mm(x, wa[c][...])
        qk = lin[:, :RW]
        rots.append((qk * cos_ref[c] + partner(qk) * sin_ref[c]).astype(BF))
        vals.append(lin[:, RW:].astype(BF))
    return x, r, rots, vals


def group_probs(g, rots, vals):
    k = pair(rots[0], rots[1], QW + g * PART)
    v = pair(vals[0], vals[1], g * PART)
    q = jnp.concatenate(
        [pair(rots[0], rots[1], (g * GROUP + i) * PART) for i in range(GROUP)], axis=0
    )
    s = mm(q, k, 1, 1) * HEAD ** (-0.5)
    tokens = k.shape[0]
    row = lax.broadcasted_iota(jnp.int32, s.shape, 0) % tokens
    col = lax.broadcasted_iota(jnp.int32, s.shape, 1)
    s = jnp.where(row >= col, s, MASKED)
    e = jnp.exp(s - jnp.max(s, axis=1, keepdims=True))
    p = e / jnp.sum(e, axis=1, keepdims=True)
    return q, k, v, p


def attn_fwd_kernel(h_ref, gain_ref, cos_ref, sin_ref, wa0, wa1, wo0, wo1, mid_ref):
    h = h_ref[...]
    tokens = h.shape[0]
    _, _, rots, vals = project(h, gain_ref[0:1, :], cos_ref, sin_ref, (wa0, wa1))
    heads = []
    for g in range(KV_HEADS):
        _, _, v, p = group_probs(g, rots, vals)
        o = mm(p.astype(BF), v).astype(BF)
        heads += [o[i * tokens : (i + 1) * tokens] for i in range(GROUP)]
    a0 = jnp.concatenate([o[:, :PART] for o in heads], axis=1)
    a1 = jnp.concatenate([o[:, PART:] for o in heads], axis=1)
    mid_ref[...] = h + mm(a0, wo0[...]) + mm(a1, wo1[...])


def mlp_fwd_kernel(mid_ref, gain_ref, wg0, wg1, wd0, wd1, out_ref, outb_ref):
    mid = mid_ref[...]
    x = (mid * gain_ref[1:2, :]).astype(BF)
    r = inv_rms(mid)
    total = mid
    for wg, wd in ((wg0, wd0), (wg1, wd1)):
        gate = r * mm(x, wg[0])
        up = r * mm(x, wg[1])
        act = (gate * jax.nn.sigmoid(gate) * up).astype(BF)
        total = total + mm(act, wd[...], 1, 1)
    out_ref[...] = total
    outb_ref[...] = total.astype(BF)


def mlp_bwd_kernel(
    mid_ref, g_ref, gain_ref, wg0, wg1, wd0, wd1, gmid_ref, *save_refs
):
    mid = mid_ref[...]
    gout = g_ref[...].astype(F32)
    gb = gout.astype(BF)
    gain = gain_ref[1:2, :]
    x = (mid * gain).astype(BF)
    r = inv_rms(mid)
    dx = None
    for c, (wg, wd) in enumerate(((wg0, wd0), (wg1, wd1))):
        gate = r * mm(x, wg[0])
        up = r * mm(x, wg[1])
        dact = mm(gb, wd[...])
        s = jax.nn.sigmoid(gate)
        silu = gate * s
        dgate = (r * (dact * up * s * (1.0 + gate * (1.0 - s)))).astype(BF)
        dup = (r * (dact * silu)).astype(BF)
        term = mm(dgate, wg[0], 1, 1) + mm(dup, wg[1], 1, 1)
        dx = term if dx is None else dx + term
        if save_refs and c == 0:
            x_ref, gb_ref, act_ref, dpm_ref, _ = save_refs
            x_ref[...] = x
            gb_ref[...] = gb
            act_ref[...] = (silu * up).astype(BF)
            dpm_ref[0] = dgate
            dpm_ref[1] = dup
    inner = jnp.sum(mid * gain * dx, axis=1, keepdims=True)
    gmid_ref[...] = gout + gain * dx - mid * (r * r * inner / D)
    if save_refs:
        save_refs[4][...] = jnp.sum(mid * dx, axis=0, keepdims=True)


def attn_bwd_kernel(
    h_ref, gmid_ref, gain_ref, cos_ref, sin_ref, wa0, wa1, wo0, wo1, gin_ref, ginb_ref, *save_refs
):
    h = h_ref[...]
    gmid = gmid_ref[...]
    gain = gain_ref[0:1, :]
    tokens = h.shape[0]
    x, r, rots, vals = project(h, gain, cos_ref, sin_ref, (wa0, wa1))
    mb = gmid.astype(BF)
    dv0 = mm(mb, wo0[...], 1, 1).astype(BF)
    dv1 = mm(mb, wo1[...], 1, 1).astype(BF)
    attn0, dq, dk, dv = [], [], [], []
    for g in range(KV_HEADS):
        q, k, v, p = group_probs(g, rots, vals)
        pb = p.astype(BF)
        do = jnp.concatenate(
            [pair(dv0, dv1, (g * GROUP + i) * PART) for i in range(GROUP)], axis=0
        )
        if save_refs:
            o = mm(pb, v).astype(BF)
            attn0 += [o[i * tokens : (i + 1) * tokens, :PART] for i in range(GROUP)]
        dv.append(mm(pb, do, 0, 0))
        dp = mm(do, v, 1, 1)
        ds = (p * (dp - jnp.sum(p * dp, axis=1, keepdims=True))).astype(BF)
        dqg = mm(ds, k) * HEAD ** (-0.5)
        dq += [dqg[i * tokens : (i + 1) * tokens] for i in range(GROUP)]
        dk.append(mm(ds, q, 0, 0) * HEAD ** (-0.5))
    dx = None
    for c, wa in enumerate((wa0, wa1)):
        piece = [y[:, c * PART : (c + 1) * PART] for y in dq + dk]
        dqk = jnp.concatenate(piece, axis=1)
        dqk = dqk * cos_ref[c] - partner(dqk) * sin_ref[c]
        dvc = jnp.concatenate([y[:, c * PART : (c + 1) * PART] for y in dv], axis=1)
        dpa = (r * jnp.concatenate([dqk, dvc], axis=1)).astype(BF)
        term = mm(dpa, wa[...], 1, 1)
        dx = term if dx is None else dx + term
        if save_refs and c == 0:
            save_refs[3][...] = dpa
    inner = jnp.sum(h * gain * dx, axis=1, keepdims=True)
    gin = gmid + gain * dx - h * (r * r * inner / D)
    gin_ref[...] = gin
    ginb_ref[...] = gin.astype(BF)
    if save_refs:
        save_refs[0][...] = x
        save_refs[1][...] = mb
        save_refs[2][...] = jnp.concatenate(attn0, axis=1)
        save_refs[4][...] = jnp.sum(h * dx, axis=0, keepdims=True)


def mlp_dw_kernel(x_ref, gb_ref, act_ref, dpm_ref, *out_refs):
    half = out_refs[0].shape[0]
    dd = mm(gb_ref[...], act_ref[...], 0, 0).astype(BF)
    dg = mm(x_ref[...], dpm_ref[0], 0, 0).astype(BF)
    du = mm(x_ref[...], dpm_ref[1], 0, 0).astype(BF)
    for i, grad in enumerate((dd, dg, du)):
        out_refs[2 * i][...] = grad[:half]
        out_refs[2 * i + 1][...] = grad[half:]


def attn_dw_kernel(x_ref, mb_ref, at_ref, dpa_ref, da_mine, da_other, do_mine, do_other):
    half = da_mine.shape[0]
    do = mm(at_ref[...], mb_ref[...], 0, 0).astype(BF)
    do_mine[...] = do[:, :half]
    do_other[...] = do[:, half:]
    da = mm(x_ref[...], dpa_ref[...], 0, 0).astype(BF)
    da_mine[...] = da[:half]
    da_other[...] = da[half:]


def call(kernel, outs, flops, *args):
    nbytes = sum(a.size * a.dtype.itemsize for a in args)
    return pl.pallas_call(
        kernel,
        out_shape=[jax.ShapeDtypeStruct(s, d) for s, d in outs],
        in_specs=[pl.BlockSpec(memory_space=pltpu.VMEM)] * len(args),
        out_specs=[pl.BlockSpec(memory_space=pltpu.VMEM)] * len(outs),
        compiler_params=pltpu.CompilerParams(vmem_limit_bytes=60 << 20),
        cost_estimate=pl.CostEstimate(
            flops=int(flops), bytes_accessed=nbytes, transcendentals=0
        ),
    )(*args)


def swap(x, axis):
    count = lax.axis_size(axis)
    return lax.ppermute(x, axis, [(i, count - 1 - i) for i in range(count)])


def sum_over(values, axis):
    count = lax.axis_size(axis)
    if count > 8 or count & (count - 1) or values.shape[0] % count:
        return lax.psum(values, axis)
    index = lax.axis_index(axis)
    bits = [1 << i for i in range(count.bit_length() - 1)]
    for bit in bits:
        rows = values.shape[0] // 2
        upper = (index // bit) % 2
        keep = lax.dynamic_slice_in_dim(values, upper * rows, rows, 0)
        send = lax.dynamic_slice_in_dim(values, (1 - upper) * rows, rows, 0)
        got = lax.ppermute(send, axis, [(i, i ^ bit) for i in range(count)])
        values = (keep.astype(F32) + got.astype(F32)).astype(BF)
    for bit in bits[::-1]:
        upper = (index // bit) % 2
        got = lax.ppermute(values, axis, [(i, i ^ bit) for i in range(count)])
        values = jnp.where(
            upper == 0,
            jnp.concatenate([values, got], axis=0),
            jnp.concatenate([got, values], axis=0),
        )
    return values


def per_device(
    hidden_in, cotangent, positions, w_query, w_keyval, w_output, w_gateup, w_down, norm_gains
):
    seqs, tokens, quarter = hidden_in.shape
    ff = w_down.shape[1]
    half = w_query.shape[1]
    assert lax.axis_size("row") == 2 and lax.axis_size("col") == 2 and seqs == 2
    section = lax.axis_index("section")
    row = lax.axis_index("row")
    col = lax.axis_index("col")
    first_col = col == 0

    both = jnp.concatenate([hidden_in, cotangent], axis=1)
    w_attn = jnp.concatenate([w_query[0, :, 0, :], w_keyval[0, :, 0, :]], axis=1)
    own = lax.dynamic_index_in_dim(both, row, 0, keepdims=False)
    away = lax.dynamic_index_in_dim(both, 1 - row, 0, keepdims=False)
    wa_got = swap(w_attn, "row")
    w_out = w_output[0, 0]
    wo_got = swap(w_out, "row")
    away = swap(away, "row")
    w_mlp, w_back, away, wa_got = lax.optimization_barrier(
        (w_gateup[0], w_down[0].T, away, wa_got)
    )
    wg_got = swap(w_mlp, "row")
    wd_got = swap(w_back, "row")
    across = jnp.concatenate([own, away], axis=0)
    beside = swap(across, "col")
    low = jnp.where(first_col, across, beside)
    high = jnp.where(first_col, beside, across)
    n2 = 2 * tokens
    full = jnp.concatenate([low[:n2], high[:n2], low[n2:], high[n2:]], axis=1)
    h0 = full[:tokens].astype(F32)
    cot = full[tokens:]

    gains = jnp.concatenate([norm_gains[0], swap(norm_gains[0], "row")], axis=1).astype(F32)
    wa0 = jnp.concatenate([w_attn, wa_got], axis=0)
    wa1 = swap(wa0, "col")
    wo0 = jnp.concatenate([w_out, wo_got], axis=1)
    wo1 = swap(wo0, "col")

    pos = lax.dynamic_index_in_dim(positions, row, 0, keepdims=False).astype(F32)
    lane = jnp.arange(PART, dtype=jnp.int32)
    cols = jnp.stack([col, 1 - col]).astype(jnp.int32)
    freq_index = (cols[:, None] * (PART // 2) + lane[None, :] % (PART // 2)).astype(F32)
    rates = jnp.exp(freq_index * (-2.0 * math.log(THETA) / HEAD))
    angles = pos[None, :, None] * rates[:, None, :]
    sign = jnp.where(lane < PART // 2, -1.0, 1.0).astype(F32)
    cos = jnp.tile(jnp.cos(angles), (1, 1, RW // PART))
    sin = jnp.tile(jnp.sin(angles) * sign, (1, 1, RW // PART))

    wa = (wa0, wa1, wo0, wo1)
    tok = (tokens, D)
    flops_a = 2 * tokens * D * (RW + KW) * 2 + 2 * tokens * D * D + 4 * tokens * tokens * D
    flops_m = 2 * tokens * D * 3 * 2 * ff

    def attn_forward(h):
        return call(attn_fwd_kernel, [(tok, F32)], flops_a, h, gains, cos, sin, *wa)[0]

    mid = attn_forward(h0)
    mid, wg_got, wd_got = lax.optimization_barrier((mid, wg_got, wd_got))
    wg0 = jnp.concatenate([w_mlp, wg_got], axis=1)
    wg1 = swap(wg0, "col")
    wd0 = jnp.concatenate([w_back, wd_got], axis=0)
    wd1 = swap(wd0, "col")
    wm = (wg0, wg1, wd0, wd1)

    def mlp_forward(mid):
        return call(mlp_fwd_kernel, [(tok, F32), (tok, BF)], flops_m, mid, gains, *wm)

    def step(x, by):
        return lax.ppermute(x, "section", [(0, 1)] if by > 0 else [(1, 0)])

    _, sent = mlp_forward(mid)
    h = jnp.where(section == 0, h0, step(sent, 1).astype(F32))
    mid = attn_forward(h)
    out, _ = mlp_forward(mid)

    gmid, = call(
        mlp_bwd_kernel, [(tok, F32)], 2.7 * flops_m, mid, cot, gains, *wm
    )
    _, ginb = call(
        attn_bwd_kernel, [(tok, F32), (tok, BF)], 3 * flops_a, h, gmid, gains, cos, sin, *wa
    )
    came, out = lax.optimization_barrier((step(ginb, -1), out))
    g = jnp.where(section == 1, cot, came)
    gmid, xm, gb, act, dpm, dgain_m = call(
        mlp_bwd_kernel,
        [
            (tok, F32),
            (tok, BF),
            (tok, BF),
            ((tokens, ff), BF),
            ((2, tokens, ff), BF),
            ((1, D), F32),
        ],
        2.7 * flops_m,
        mid,
        g,
        gains,
        *wm,
    )
    dd_mine, dd_other, dg_mine, dg_other, du_mine, du_other = call(
        mlp_dw_kernel,
        [((half, ff), BF)] * 6,
        flops_m // 2,
        xm,
        gb,
        act,
        dpm,
    )
    dd_got, dg_got, du_got = [swap(x, "row") for x in (dd_other, dg_other, du_other)]
    gmid, dd_other, dg_other, du_other = lax.optimization_barrier(
        (gmid, dd_other, dg_other, du_other)
    )
    gin, _, xa, mb, at0, dpa, dgain_a = call(
        attn_bwd_kernel,
        [
            (tok, F32),
            (tok, BF),
            (tok, BF),
            (tok, BF),
            ((tokens, QW), BF),
            ((tokens, RW + KW), BF),
            ((1, D), F32),
        ],
        3 * flops_a,
        h,
        gmid,
        gains,
        cos,
        sin,
        *wa,
    )
    da_mine, da_other, do_mine, do_other = call(
        attn_dw_kernel,
        [((half, RW + KW), BF)] * 2 + [((QW, half), BF)] * 2,
        flops_a // 2,
        xa,
        mb,
        at0,
        dpa,
    )

    def joined(mine, got):
        return (mine.astype(F32) + got.astype(F32)).astype(BF)

    early = jnp.concatenate([joined(dd_mine, dd_got), joined(dg_mine, dg_got)], axis=1)
    early, da_other, do_other, gin, dgain_a = lax.optimization_barrier(
        (early, da_other, do_other, gin, dgain_a)
    )
    da_got, do_got = swap(da_other, "row"), swap(do_other, "row")
    dgain = jnp.concatenate([dgain_a, dgain_m], axis=0)
    dgain = dgain[:, :half] + swap(dgain[:, half:], "row")
    dgain = jnp.where(first_col, dgain[:, :quarter], dgain[:, quarter:]).astype(BF)
    late = jnp.concatenate(
        [
            joined(du_mine, du_got),
            joined(da_mine, da_got),
            joined(do_mine, do_got),
            dgain.reshape(half, 1),
        ],
        axis=1,
    )
    early = sum_over(early, "dp")
    late = sum_over(late, "dp")
    dd, dg = early[:, :ff], early[:, ff:]
    du, da = late[:, :ff], late[:, ff : ff + RW + KW]
    do, dn = late[:, ff + RW + KW : -1], late[:, -1].reshape(2, quarter)

    def home(x):
        mine = jnp.where(first_col, x[:, :quarter], x[:, quarter:half])
        other = jnp.where(first_col, x[:, half : half + quarter], x[:, half + quarter :])
        got = swap(other.astype(BF), "row").astype(F32)
        return jnp.where(row == 0, jnp.stack([mine, got]), jnp.stack([got, mine]))[None]

    return (
        home(out),
        home(gin),
        da[:, :QW].astype(F32).reshape(1, half, 1, QW),
        da[:, QW:].astype(F32).reshape(1, half, 1, 2 * KW),
        do.astype(F32)[None, None],
        jnp.stack([dg, du]).astype(F32)[None],
        dd.astype(F32).T[None],
        dn.astype(F32)[None],
    )


def solution(mesh):
    return jax.shard_map(
        per_device,
        mesh=mesh,
        in_specs=(
            P("dp", None, ("row", "col")),
            P("dp", None, ("row", "col")),
            P("dp", None),
            P("section", "row", "col", None),
            P("section", "row", "col", None),
            P("section", "col", None, "row"),
            P("section", None, "row", "col"),
            P("section", "col", "row"),
            P("section", None, "row"),
        ),
        out_specs=(
            P("section", "dp", None, ("row", "col")),
            P("section", "dp", None, ("row", "col")),
            P("section", "row", "col", None),
            P("section", "row", "col", None),
            P("section", "col", None, "row"),
            P("section", None, "row", "col"),
            P("section", "col", "row"),
            P("section", None, ("row", "col")),
        ),
        check_vma=False,
    )
```
